32 devices in a mesh: cons: 4 (over y, core), prod: 8 (over z, x).
Axes of the slice: x: 2, y: 2, z: 4, core: 2. Of those that a mesh axis runs over, the one named last changes fastest.
Arguments:
- tastes: bfloat16 [16384, 128], P('cons'), may hold values from -128 to 128
- price_coef: float32 [16384], P('cons'), may hold values from 0.5 to 5
- characteristics: bfloat16 [16384, 128], P('prod'), may hold values from -6 to 6
- mean_utility: float32 [16384], P('prod'), may hold values from -4 to 4
- panel_cols: int32 [256], replicated, may hold values from 0 to 16383
- firm_map: int32 [16384], P('prod'), may hold values from 0 to 16383, as said below
- inverses: float32 [128, 128, 128], P('prod'), may hold values from -0.5 to 0.5
Outputs:
- shares: float32 [16384], P('prod')
- markup: float32 [16384], P('prod')
- response: float32 [16384, 256], P('prod')
The draws below stay inside these ranges and needn't reach their ends.
Inputs may be any that keep to these rules, and one draw needn't show every extreme that they name: `firm_map`: a permutation of the products; the rows of firm order held by each index of prod name exactly 256 products held by each index of prod.
All inputs are finite; a program needn't handle non-finite values.
Results may differ from the reference program's by a relative error of at most 0.002.
The reference program's roundings to bfloat16 on the way count: a program that leaves them out, or rounds other values in their place, can miss the bound.
Values may be sent and summed in bfloat16 or wider, within the bound.
A program may use at most 64 MiB of HBM per device.

```python
import math
import jax
import jax.numpy as jnp
from jax import lax

K = 128
COLS = 256
B = 128
JD = 2048
J = 16384
I = 16384
F = 128


def drawn_draws(key):
    key_chars, key_tastes = jax.random.split(jax.random.fold_in(key, 7), 2)
    chars_all = jnp.clip(jax.random.normal(key_chars, (J, K), jnp.float32), -6.0, 6.0)
    tastes_all = jnp.clip(jax.random.normal(key_tastes, (I, K), jnp.float32), -6.0, 6.0) * (3.0 / math.sqrt(K))
    return (chars_all, tastes_all)


def draw_characteristics(key, part):
    return drawn_draws(key)[0].astype(jnp.bfloat16)


def draw_tastes(key, part):
    return drawn_draws(key)[1].astype(jnp.bfloat16)


def shuffle_one(subkey):
    return jax.random.permutation(subkey, JD).astype(jnp.int32)


def draw_firm_map(key, part):
    sources = J // JD
    per_pair = JD // sources
    key_first, key_second = jax.random.split(jax.random.fold_in(key, 11))
    shuffled = jax.vmap(shuffle_one)(jax.random.split(key_first, sources))
    owned = shuffled + (jnp.arange(sources, dtype=jnp.int32) * JD)[:, None]
    routed = owned.reshape(sources, sources, per_pair).transpose(1, 0, 2).reshape(sources, JD)
    mixing = jax.vmap(shuffle_one)(jax.random.split(key_second, sources))
    mixed = jnp.take_along_axis(routed, mixing, axis=1)
    return mixed.reshape(J).astype(jnp.int32)


def with_ends(result, rng, smallest, top_value):
    longest = result.shape.index(max(result.shape))
    spots = []
    for shift in (0, 1):
        where = [jax.random.randint(jax.random.fold_in(rng, axis), (), 0, length) for axis, length in enumerate(result.shape)]
        where[longest] = (where[longest] + shift) % result.shape[longest]
        spots.append(tuple(where))
    return result.at[spots[0]].set(smallest).at[spots[1]].set(top_value)


def block_scale(own_key, extent, shards, least, largest):
    gain = 1.0
    for position, shards_of in shards:
        steps = jax.random.uniform(jax.random.fold_in(jax.random.fold_in(own_key, 6), position), (shards_of,), jnp.float32, least / len(shards), largest / len(shards))
        gain = gain * jnp.repeat(jnp.exp(steps), extent[position] // shards_of).reshape((-1,) + (1,) * (len(extent) - 1 - position))
    return gain


def gaussian(stream_key, shape, scale, most, cuts=(), held_as=jnp.bfloat16):
    drawn = scale * jax.random.normal(stream_key, shape, jnp.float32)
    if cuts:
        drawn = drawn * block_scale(stream_key, shape, cuts, -0.22, 0.18)
    return jnp.clip(drawn, -most, most).astype(held_as)


def setup_inputs(seed: int = 0) -> dict:
    streams_of = jax.random.split(jax.random.key(seed), 8)
    return {
        "tastes": draw_tastes(jax.random.fold_in(streams_of[7], 71), 0),
        "price_coef": jnp.clip(jnp.exp(math.log(5.0) - 2.3025851 * jax.random.uniform(streams_of[1], (I,), jnp.float32) ** block_scale(streams_of[1], (I,), ((0, 4),), -0.2, 0.2)), 0.5, 5.0),
        "characteristics": draw_characteristics(jax.random.fold_in(streams_of[7], 71), 0),
        "mean_utility": gaussian(streams_of[3], (J,), 1.0, 4.0, ((0, 8),), jnp.float32),
        "panel_cols": with_ends(jax.random.randint(streams_of[4], (COLS,), 0, J), jax.random.fold_in(streams_of[4], 1), 0, J - 1).astype(jnp.int32),
        "firm_map": draw_firm_map(jax.random.fold_in(streams_of[7], 71), 0),
        "inverses": gaussian(streams_of[6], (F, B, B), B ** -0.5, 0.5, ((0, 8),), jnp.float32),
    }


def reference(tastes, price_coef, characteristics, mean_utility, panel_cols, firm_map, inverses):
    count_products = characteristics.shape[0]
    count_consumers = tastes.shape[0]
    block_rows = min(512, count_consumers)
    block_count = count_consumers // block_rows
    col_chars = characteristics[panel_cols]
    col_means = mean_utility[panel_cols]
    taste_blocks = tastes.reshape(block_count, block_rows, tastes.shape[1])
    coef_blocks = price_coef.reshape(block_count, block_rows)

    def consume(state_now, inputs):
        panel_sum, share_sum, diag_sum = state_now
        taste_block, coef_block = inputs
        utility = jnp.dot(taste_block, characteristics.T, preferred_element_type=jnp.float32) + mean_utility[None, :]
        highest = jnp.maximum(jnp.max(utility, axis=1), 0.0)
        exponent = jnp.exp(utility - highest[:, None])
        denominator = jnp.exp(-highest) + jnp.sum(exponent, axis=1)
        scaled = count_products * exponent / denominator[:, None]
        share_sum = share_sum + jnp.sum(scaled, axis=0)
        diag_sum = diag_sum + jnp.dot(coef_block, scaled, precision=lax.Precision.HIGHEST)
        col_util = jnp.dot(taste_block, col_chars.T, preferred_element_type=jnp.float32) + col_means[None, :]
        col_scaled = count_products * jnp.exp(col_util - highest[:, None]) / denominator[:, None]
        weighted = (coef_block[:, None] * col_scaled).astype(jnp.bfloat16)
        panel_sum = panel_sum + lax.dot_general(scaled.astype(jnp.bfloat16), weighted, (((0,), (0,)), ((), ())), preferred_element_type=jnp.float32)
        return (panel_sum, share_sum, diag_sum), None

    start_state = (jnp.zeros((count_products, panel_cols.shape[0]), jnp.float32), jnp.zeros((count_products,), jnp.float32), jnp.zeros((count_products,), jnp.float32))
    (panel_sum, share_sum, diag_sum), _ = lax.scan(consume, start_state, (taste_blocks, coef_blocks))
    cross = panel_sum / count_consumers
    shares = share_sum / count_consumers
    diagonal = diag_sum / count_consumers
    product_ids = jnp.arange(count_products, dtype=jnp.int32)
    marks = (product_ids[:, None] == panel_cols[None, :]).astype(jnp.float32)
    jacobian = cross - diagonal[:, None] * marks
    block_size = inverses.shape[1]
    firm_count = inverses.shape[0]
    ordered = jacobian[firm_map].reshape(firm_count, block_size, panel_cols.shape[0])
    response = jnp.einsum("fab,fbc->fac", inverses, ordered, precision=lax.Precision.HIGHEST).reshape(count_products, panel_cols.shape[0])
    ordered_shares = shares[firm_map].reshape(firm_count, block_size)
    markup = jnp.einsum("fab,fb->fa", inverses, ordered_shares, precision=lax.Precision.HIGHEST).reshape(count_products)
    return shares, markup, response
```

```python
import functools
import jax
import jax.numpy as jnp
from jax import lax
from jax.experimental import pallas as pl
from jax.experimental.pallas import tpu as pltpu
from jax.sharding import PartitionSpec as P

F32 = jnp.float32
BF16 = jnp.bfloat16
NT = (((1,), (1,)), ((), ()))
MESH = pl.DeviceIdType.MESH
VMEM = pl.BlockSpec(memory_space=pltpu.VMEM)
LIMIT = 63 * 1024 * 1024


def exchange_kernel(n, x_ref, o_ref, ssem, rsem, lsem):
    me = lax.axis_index("prod")
    barrier = pltpu.get_barrier_semaphore()
    for d in range(1, n):
        pl.semaphore_signal(barrier, inc=1, device_id={"prod": lax.rem(me + d, n)}, device_id_type=MESH)
    pl.semaphore_wait(barrier, n - 1)
    copies = []
    for d in range(1, n):
        peer = lax.rem(me + d, n)
        copy = pltpu.make_async_remote_copy(
            x_ref.at[peer], o_ref.at[me], ssem.at[d], rsem.at[d],
            device_id={"prod": peer}, device_id_type=MESH,
        )
        copy.start()
        copies.append(copy)
    own = pltpu.make_async_copy(x_ref.at[me], o_ref.at[me], lsem)
    own.start()
    own.wait()
    for copy in copies:
        copy.wait()


def exchange(x, cid):
    n = x.shape[0]
    return pl.pallas_call(
        functools.partial(exchange_kernel, n),
        out_shape=jax.ShapeDtypeStruct(x.shape, x.dtype),
        in_specs=[VMEM],
        out_specs=VMEM,
        scratch_shapes=[
            pltpu.SemaphoreType.DMA((n,)),
            pltpu.SemaphoreType.DMA((n,)),
            pltpu.SemaphoreType.DMA(()),
        ],
        compiler_params=pltpu.CompilerParams(collective_id=cid, has_side_effects=True),
    )(x)


def main_kernel(
    n, count_products, count_consumers, IC, JT,
    C, T, coef, colpart, inv, ids, cols,
    out, sm,
    E, MS, CC, FL, WT, PO, PX, PR, YS, YR, ST,
    ms_s, ms_r, cc_s, cc_r, px_s, px_r, y_s, y_r, st_s, st_r, o_s, o_r,
):
    me = lax.axis_index("prod")
    cons = lax.axis_index("cons")
    core = lax.rem(cons, 2)
    partner = cons + 1 - 2 * core
    across = lax.rem(cons + 2, 4)
    LP = C.shape[0]
    LI = T.shape[0]
    nc, nt = LI // IC, LP // JT
    half = out.shape[1] // 2
    block = inv.shape[1]

    barrier = pltpu.get_barrier_semaphore()
    for d in range(1, n):
        pl.semaphore_signal(barrier, inc=1, device_id={"prod": lax.rem(me + d, n)}, device_id_type=MESH)
    for d in range(1, 4):
        pl.semaphore_signal(barrier, inc=1, device_id={"cons": lax.rem(cons + d, 4)}, device_id_type=MESH)
    pl.semaphore_wait(barrier, n + 2)

    def cc_copy(d):
        return pltpu.make_async_remote_copy(
            colpart, CC.at[me], cc_s.at[d], cc_r.at[d],
            device_id={"prod": lax.rem(me + d, n)}, device_id_type=MESH,
        )

    def ms_copy(d, ic):
        return pltpu.make_async_remote_copy(
            MS.at[0, ic], MS.at[d, ic], ms_s.at[d, ic], ms_r.at[d, ic],
            device_id={"prod": lax.rem(me + d, n)}, device_id_type=MESH,
        )

    def each_peer(fn):
        def step(d, carry):
            fn(d)
            return carry
        lax.fori_loop(1, n, step, 0)

    each_peer(lambda d: cc_copy(d).start())
    CC[me] = colpart[...]

    def pass_one(ic, carry):
        i0 = pl.multiple_of(ic * IC, IC)
        tb = T[pl.ds(i0, IC), :]

        def utility(jt, m8):
            rows = pl.ds(pl.multiple_of(jt * JT, JT), JT)
            u = lax.dot_general(C[rows, :], tb, NT, preferred_element_type=F32)
            E[rows, pl.ds(i0, IC)] = u
            return jnp.maximum(m8, jnp.max(u.reshape(JT // 8, 8, IC), axis=0))

        m8 = lax.fori_loop(0, nt, utility, jnp.zeros((8, IC), F32))
        m = jnp.max(m8, axis=0, keepdims=True)

        def expo(jt, s8):
            rows = pl.ds(pl.multiple_of(jt * JT, JT), JT)
            e = jnp.exp(E[rows, pl.ds(i0, IC)] - m)
            E[rows, pl.ds(i0, IC)] = e
            return s8 + jnp.sum(e.reshape(JT // 8, 8, IC), axis=0)

        s8 = lax.fori_loop(0, nt, expo, jnp.zeros((8, IC), F32))
        MS[0, ic, 0:1, :] = m
        MS[0, ic, 1:2, :] = jnp.sum(s8, axis=0, keepdims=True)
        each_peer(lambda d: ms_copy(d, ic).start())
        return carry

    lax.fori_loop(0, nc, pass_one, 0)
    each_peer(lambda d: cc_copy(d).wait())
    ccv = CC[...].reshape(CC.shape[0] * CC.shape[1], CC.shape[2]).astype(BF16)

    def weights(ic, carry):
        each_peer(lambda d: ms_copy(d, ic).wait())
        i0 = pl.multiple_of(ic * IC, IC)
        peak = MS[0, ic, 0:1, :]
        for d in range(1, n):
            peak = jnp.maximum(peak, MS[d, ic, 0:1, :])
        den = jnp.exp(-peak)
        for d in range(n):
            den = den + MS[d, ic, 1:2, :] * jnp.exp(MS[d, ic, 0:1, :] - peak)
        f = count_products / den
        FL[:, pl.ds(i0, IC)] = jnp.exp(MS[0, ic, 0:1, :] - peak) * f
        cu = lax.dot_general(ccv, T[pl.ds(i0, IC), :], NT, preferred_element_type=F32)
        w = coef[:, pl.ds(i0, IC)] * (f * jnp.exp(cu - peak))
        WT[pl.ds(i0, IC), :] = w.T.astype(BF16)
        return carry

    lax.fori_loop(0, nc, weights, 0)

    def px_copy(jt):
        rows = pl.ds(pl.multiple_of(jt * JT, JT), JT)
        return pltpu.make_async_remote_copy(
            PX.at[rows], PR.at[rows], px_s.at[jt], px_r.at[jt],
            device_id={"cons": partner}, device_id_type=MESH,
        )

    def y_copy(jt):
        rows = pl.ds(pl.multiple_of(jt * JT, JT), JT)
        return pltpu.make_async_remote_copy(
            YS.at[rows], YR.at[rows], y_s.at[jt], y_r.at[jt],
            device_id={"cons": across}, device_id_type=MESH,
        )

    def o_copy(jt):
        rows = pl.ds(pl.multiple_of(jt * JT, JT), JT)
        mine = pl.ds(pl.multiple_of(core * half, half), half)
        return pltpu.make_async_remote_copy(
            out.at[rows, mine], out.at[rows, mine], o_s.at[jt], o_r.at[jt],
            device_id={"cons": partner}, device_id_type=MESH,
        )

    def st_copy(d):
        return pltpu.make_async_remote_copy(
            ST.at[cons], ST.at[cons], st_s.at[d], st_r.at[d],
            device_id={"cons": lax.rem(cons + d, 4)}, device_id_type=MESH,
        )

    def forward(jt):
        rows = pl.ds(pl.multiple_of(jt * JT, JT), JT)
        px_copy(jt).wait()
        YS[rows, :] = (PO[rows, :] + PR[rows, :]).astype(BF16)
        y_copy(jt).start()

    def panel(jt, carry):
        rows = pl.ds(pl.multiple_of(jt * JT, JT), JT)

        def over(ic, state):
            acc, sh, dg = state
            i0 = pl.multiple_of(ic * IC, IC)
            sc = E[rows, pl.ds(i0, IC)] * FL[:, pl.ds(i0, IC)]
            acc = acc + jnp.dot(sc.astype(BF16), WT[pl.ds(i0, IC), :], preferred_element_type=F32)
            cs = sc * coef[:, pl.ds(i0, IC)]
            for b in range(IC // 128):
                sh = sh + sc[:, b * 128:(b + 1) * 128]
                dg = dg + cs[:, b * 128:(b + 1) * 128]
            return acc, sh, dg

        zero = jnp.zeros((JT, 128), F32)
        acc, sh, dg = lax.fori_loop(0, nc, over, (jnp.zeros((JT, 2 * half), F32), zero, zero))
        first, second = acc[:, :half], acc[:, half:]
        PO[rows, :] = jnp.where(core == 0, first, second)
        PX[rows, :] = jnp.where(core == 0, second, first)
        px_copy(jt).start()
        ST[cons, 0:1, rows] = jnp.sum(sh.T, axis=0, keepdims=True)
        ST[cons, 1:2, rows] = jnp.sum(dg.T, axis=0, keepdims=True)

        @pl.when(jt > 0)
        def _():
            forward(jt - 1)

        return carry

    lax.fori_loop(0, nt, panel, 0)
    for d in range(1, 4):
        st_copy(d).start()
    forward(nt - 1)
    for d in range(1, 4):
        st_copy(d).wait()
    sm[0:1, :] = (ST[0, 0:1, :] + ST[1, 0:1, :] + ST[2, 0:1, :] + ST[3, 0:1, :]) / count_consumers
    ST[0, 1:2, :] = (ST[0, 1:2, :] + ST[1, 1:2, :] + ST[2, 1:2, :] + ST[3, 1:2, :]) / count_consumers
    mine = pl.ds(pl.multiple_of(core * half, half), half)
    heads = cols[:, mine]

    def finish(jt, carry):
        y_copy(jt).wait()
        for b in range(JT // block):
            r0 = pl.multiple_of(jt * JT + b * block, block)
            rows = pl.ds(r0, block)
            fb = jt * (JT // block) + b
            x = (YS[rows, :].astype(F32) + YR[rows, :].astype(F32)) / count_consumers
            diag = jnp.broadcast_to(ST[0, 1:2, rows], (half, block)).T
            jac = x - jnp.where(ids[rows, :] == heads, diag, 0.0)
            m = inv[fb]
            out[rows, mine] = jnp.dot(m, jac, precision=lax.Precision.HIGHEST, preferred_element_type=F32)
            share8 = jnp.broadcast_to(sm[0:1, rows], (8, block))
            mk = lax.dot_general(share8, m, NT, precision=lax.Precision.HIGHEST, preferred_element_type=F32)
            sm[1:2, rows] = mk[0:1, :]
        o_copy(jt).start()
        return carry

    lax.fori_loop(0, nt, finish, 0)

    def drain(jt, carry):
        o_copy(jt).wait()
        return carry

    lax.fori_loop(0, nt, drain, 0)


def run_main(n, caug, taug, coef, colpart, inverses, ids, cols, count_products, count_consumers):
    LP, LI, W = caug.shape[0], taug.shape[0], cols.shape[1]
    KA = caug.shape[1]
    IC, JT = min(512, LI), min(256, LP)
    nc, nt = LI // IC, LP // JT
    half = W // 2
    dma = pltpu.SemaphoreType.DMA
    return pl.pallas_call(
        functools.partial(main_kernel, n, float(count_products), float(count_consumers), IC, JT),
        out_shape=(jax.ShapeDtypeStruct((LP, W), F32), jax.ShapeDtypeStruct((2, LP), F32)),
        in_specs=[VMEM] * 7,
        out_specs=(VMEM, VMEM),
        scratch_shapes=[
            pltpu.VMEM((LP, LI), F32),
            pltpu.VMEM((n, nc, 2, IC), F32),
            pltpu.VMEM((n, W // n, KA), F32),
            pltpu.VMEM((1, LI), F32),
            pltpu.VMEM((LI, W), BF16),
            pltpu.VMEM((LP, half), F32),
            pltpu.VMEM((LP, half), F32),
            pltpu.VMEM((LP, half), F32),
            pltpu.VMEM((LP, half), BF16),
            pltpu.VMEM((LP, half), BF16),
            pltpu.VMEM((4, 2, LP), F32),
            dma((n, nc)), dma((n, nc)), dma((n,)), dma((n,)),
            dma((nt,)), dma((nt,)), dma((nt,)), dma((nt,)),
            dma((4,)), dma((4,)), dma((nt,)), dma((nt,)),
        ],
        compiler_params=pltpu.CompilerParams(
            collective_id=7, has_side_effects=True, vmem_limit_bytes=LIMIT
        ),
    )(caug, taug, coef, colpart, inverses, ids, cols)


def split_mean(mean):
    a = lax.reduce_precision(mean, 8, 7)
    b = lax.reduce_precision(mean - a, 8, 7)
    c = mean - a - b
    return jnp.stack([a.astype(BF16), b.astype(BF16), c.astype(BF16)], axis=1)


def lanes(count):
    return -(-count // 128) * 128


def body(tastes, price_coef, characteristics, mean_utility, panel_cols, firm_map, inverses):
    n = lax.axis_size("prod")
    LP, K = characteristics.shape
    LI = tastes.shape[0]
    W = panel_cols.shape[0]
    count_products = LP * n
    count_consumers = LI * lax.axis_size("cons")
    pp, cp = LP // n, W // n
    KA = 2 * K
    base = lax.axis_index("prod") * LP
    local = lax.iota(jnp.int32, LP)

    sid = lax.sort(firm_map)
    wanted = jnp.pad(sid.reshape(n, 1, pp), ((0, 0), (0, 0), (0, lanes(pp) - pp)))
    asked = exchange(wanted, 1)[:, 0, :pp].reshape(LP) - base

    caug = jnp.concatenate(
        [characteristics, split_mean(mean_utility), jnp.zeros((LP, KA - K - 3), BF16)], axis=1
    )
    picks = jnp.concatenate([asked, panel_cols - base])
    hot = (picks[:, None] == local[None, :]).astype(BF16)
    got = jnp.dot(hot, caug, preferred_element_type=F32).astype(BF16)
    mine = jnp.concatenate([got[:LP].reshape(n, pp, KA), got[LP:].reshape(n, cp, KA)], axis=1)
    each = pp + cp
    wide = lanes(each)
    means = jnp.pad(mine[:, :, K:K + 3].transpose(0, 2, 1), ((0, 0), (0, 0), (0, wide - each)))
    means = means.reshape(n, 3 * wide // 128, 128)
    total = each + means.shape[1]
    fill = -(-total // 16) * 16 - total
    sent = jnp.concatenate([mine[:, :, :K], means, jnp.zeros((n, fill, K), BF16)], axis=1)
    back = exchange(sent, 2)
    means_back = back[:, each:total].reshape(n, 3, wide)[:, :, :each].transpose(0, 2, 1)
    both = jnp.concatenate([back[:, :each], means_back, jnp.zeros((n, each, KA - K - 3), BF16)], axis=2)
    colpart = jnp.sum(both[:, pp:].astype(F32), axis=0)
    turn = (firm_map[:, None] == sid[None, :]).astype(BF16)
    cfirm = jnp.dot(turn, both[:, :pp].reshape(LP, KA), preferred_element_type=F32).astype(BF16)
    taug = jnp.concatenate(
        [tastes, jnp.ones((LI, 3), BF16), jnp.zeros((LI, KA - K - 3), BF16)], axis=1
    )
    response, sm = run_main(
        n, cfirm, taug, price_coef[None, :], colpart, inverses,
        firm_map[:, None], panel_cols[None, :], count_products, count_consumers,
    )
    values = jnp.sum(jnp.where(firm_map[:, None] == sid[None, :], sm[0][:, None], 0.0), axis=0)
    values = jnp.pad(values.reshape(n, 1, pp), ((0, 0), (0, 0), (0, lanes(pp) - pp)))
    home = exchange(values, 3)[:, 0, :pp].reshape(LP)
    shares = jnp.sum(jnp.where(asked[:, None] == local[None, :], home[:, None], 0.0), axis=0)
    return shares, sm[1], response


def solution(mesh):
    return jax.shard_map(
        body,
        mesh=mesh,
        in_specs=(
            P("cons", None),
            P("cons"),
            P("prod", None),
            P("prod"),
            P(),
            P("prod"),
            P("prod", None, None),
        ),
        out_specs=(P("prod"), P("prod"), P("prod", None)),
        check_vma=False,
    )
```

```python
import functools
import jax
import jax.numpy as jnp
from jax import lax
from jax.experimental import pallas as pl
from jax.experimental.pallas import tpu as pltpu
from jax.sharding import PartitionSpec as P

F32 = jnp.float32
BF16 = jnp.bfloat16
NT = (((1,), (1,)), ((), ()))
MESH = pl.DeviceIdType.MESH
VMEM = pl.BlockSpec(memory_space=pltpu.VMEM)
LIMIT = 63 * 1024 * 1024


def exchange_kernel(n, x_ref, o_ref, ssem, rsem, lsem):
    me = lax.axis_index("prod")
    barrier = pltpu.get_barrier_semaphore()
    for d in range(1, n):
        pl.semaphore_signal(barrier, inc=1, device_id={"prod": lax.rem(me + d, n)}, device_id_type=MESH)
    pl.semaphore_wait(barrier, n - 1)
    copies = []
    for d in range(1, n):
        peer = lax.rem(me + d, n)
        copy = pltpu.make_async_remote_copy(
            x_ref.at[peer], o_ref.at[me], ssem.at[d], rsem.at[d],
            device_id={"prod": peer}, device_id_type=MESH,
        )
        copy.start()
        copies.append(copy)
    own = pltpu.make_async_copy(x_ref.at[me], o_ref.at[me], lsem)
    own.start()
    own.wait()
    for copy in copies:
        copy.wait()


def exchange(x, cid):
    n = x.shape[0]
    return pl.pallas_call(
        functools.partial(exchange_kernel, n),
        out_shape=jax.ShapeDtypeStruct(x.shape, x.dtype),
        in_specs=[VMEM],
        out_specs=VMEM,
        scratch_shapes=[
            pltpu.SemaphoreType.DMA((n,)),
            pltpu.SemaphoreType.DMA((n,)),
            pltpu.SemaphoreType.DMA(()),
        ],
        compiler_params=pltpu.CompilerParams(collective_id=cid, has_side_effects=True),
    )(x)


def shared_exchange_kernel(n, x_ref, o_ref, ssem, rsem, fs, fr, lsem):
    me = lax.axis_index("prod")
    cons = lax.axis_index("cons")
    core = lax.rem(cons, 2)
    partner = cons + 1 - 2 * core
    span = x_ref.shape[1] // 2
    part = pl.ds(pl.multiple_of(core * span, span), span)
    barrier = pltpu.get_barrier_semaphore()
    for d in range(1, n):
        pl.semaphore_signal(barrier, inc=1, device_id={"prod": lax.rem(me + d, n)}, device_id_type=MESH)
    pl.semaphore_signal(barrier, inc=1, device_id={"cons": partner}, device_id_type=MESH)
    pl.semaphore_wait(barrier, n)
    copies = []
    for d in range(1, n):
        peer = lax.rem(me + d, n)
        copy = pltpu.make_async_remote_copy(
            x_ref.at[peer, part], o_ref.at[me, part], ssem.at[d], rsem.at[d],
            device_id={"prod": peer}, device_id_type=MESH,
        )
        copy.start()
        copies.append(copy)
    own = pltpu.make_async_copy(x_ref.at[me], o_ref.at[me], lsem)
    own.start()
    passed = []
    for d in range(1, n):
        copies[d - 1].wait()
        source = lax.rem(me + n - d, n)
        copy = pltpu.make_async_remote_copy(
            o_ref.at[source, part], o_ref.at[source, part], fs.at[d], fr.at[d],
            device_id={"cons": partner}, device_id_type=MESH,
        )
        copy.start()
        passed.append(copy)
    own.wait()
    for copy in passed:
        copy.wait()


def shared_exchange(x, cid):
    n = x.shape[0]
    return pl.pallas_call(
        functools.partial(shared_exchange_kernel, n),
        out_shape=jax.ShapeDtypeStruct(x.shape, x.dtype),
        in_specs=[VMEM],
        out_specs=VMEM,
        scratch_shapes=[pltpu.SemaphoreType.DMA((n,))] * 4 + [pltpu.SemaphoreType.DMA(())],
        compiler_params=pltpu.CompilerParams(collective_id=cid, has_side_effects=True),
    )(x)


def main_kernel(
    n, count_products, count_consumers, IC, JT, GR,
    C, tastes, coef, colpart, inv, ids, cols,
    out, sm,
    T, SCB, SH, DG, E, MS, CC, FL, WT, PO, PX, PR, YS, YR, ST,
    ms_s, ms_r, cc_s, cc_r, px_s, px_r, y_s, y_r, st_s, st_r, o_s, o_r,
):
    me = lax.axis_index("prod")
    cons = lax.axis_index("cons")
    core = lax.rem(cons, 2)
    partner = cons + 1 - 2 * core
    across = lax.rem(cons + 2, 4)
    LP = C.shape[0]
    LI, K = tastes.shape
    nc, nt = LI // IC, LP // JT
    half = out.shape[1] // 2
    block = inv.shape[1]

    barrier = pltpu.get_barrier_semaphore()
    for d in range(1, n):
        pl.semaphore_signal(barrier, inc=1, device_id={"prod": lax.rem(me + d, n)}, device_id_type=MESH)
    for d in range(1, 4):
        pl.semaphore_signal(barrier, inc=1, device_id={"cons": lax.rem(cons + d, 4)}, device_id_type=MESH)
    pl.semaphore_wait(barrier, n + 2)

    def cc_copy(d):
        return pltpu.make_async_remote_copy(
            colpart, CC.at[me], cc_s.at[d], cc_r.at[d],
            device_id={"prod": lax.rem(me + d, n)}, device_id_type=MESH,
        )

    def ms_copy(d, ic):
        return pltpu.make_async_remote_copy(
            MS.at[0, ic], MS.at[d, ic], ms_s.at[d, ic], ms_r.at[d, ic],
            device_id={"prod": lax.rem(me + d, n)}, device_id_type=MESH,
        )

    def each_peer(fn):
        def step(d, carry):
            fn(d)
            return carry
        lax.fori_loop(1, n, step, 0)

    each_peer(lambda d: cc_copy(d).start())
    T[:, :K] = tastes[...]
    lane = lax.broadcasted_iota(jnp.int32, (LI, C.shape[1] - K), 1)
    T[:, K:] = jnp.where(lane < 3, 1.0, 0.0).astype(BF16)
    CC[me] = colpart[...]

    def pass_one(ic, carry):
        i0 = pl.multiple_of(ic * IC, IC)
        tb = T[pl.ds(i0, IC), :]

        def utility(jt, m8):
            rows = pl.ds(pl.multiple_of(jt * JT, JT), JT)
            u = lax.dot_general(C[rows, :], tb, NT, preferred_element_type=F32)
            E[rows, pl.ds(i0, IC)] = u
            return jnp.maximum(m8, jnp.max(u.reshape(JT // 8, 8, IC), axis=0))

        m8 = lax.fori_loop(0, nt, utility, jnp.zeros((8, IC), F32))
        m = jnp.max(m8, axis=0, keepdims=True)

        def expo(jt, s8):
            rows = pl.ds(pl.multiple_of(jt * JT, JT), JT)
            e = jnp.exp(E[rows, pl.ds(i0, IC)] - m)
            E[rows, pl.ds(i0, IC)] = e
            return s8 + jnp.sum(e.reshape(JT // 8, 8, IC), axis=0)

        s8 = lax.fori_loop(0, nt, expo, jnp.zeros((8, IC), F32))
        MS[0, ic, 0:1, :] = m
        MS[0, ic, 1:2, :] = jnp.sum(s8, axis=0, keepdims=True)
        each_peer(lambda d: ms_copy(d, ic).start())
        return carry

    lax.fori_loop(0, nc, pass_one, 0)
    each_peer(lambda d: cc_copy(d).wait())
    ccv = CC[...].reshape(CC.shape[0] * CC.shape[1], CC.shape[2]).astype(BF16)

    def weights(ic, carry):
        each_peer(lambda d: ms_copy(d, ic).wait())
        i0 = pl.multiple_of(ic * IC, IC)
        peak = MS[0, ic, 0:1, :]
        for d in range(1, n):
            peak = jnp.maximum(peak, MS[d, ic, 0:1, :])
        den = jnp.exp(-peak)
        for d in range(n):
            den = den + MS[d, ic, 1:2, :] * jnp.exp(MS[d, ic, 0:1, :] - peak)
        f = count_products / den
        FL[:, pl.ds(i0, IC)] = jnp.exp(MS[0, ic, 0:1, :] - peak) * f
        cu = lax.dot_general(ccv, T[pl.ds(i0, IC), :], NT, preferred_element_type=F32)
        w = coef[:, pl.ds(i0, IC)] * (f * jnp.exp(cu - peak))
        WT[pl.ds(i0, IC), :] = w.T.astype(BF16)
        return carry

    lax.fori_loop(0, nc, weights, 0)

    def px_copy(jt):
        rows = pl.ds(pl.multiple_of(jt * JT, JT), JT)
        return pltpu.make_async_remote_copy(
            PX.at[rows], PR.at[rows], px_s.at[jt], px_r.at[jt],
            device_id={"cons": partner}, device_id_type=MESH,
        )

    def y_copy(jt):
        rows = pl.ds(pl.multiple_of(jt * JT, JT), JT)
        return pltpu.make_async_remote_copy(
            YS.at[rows], YR.at[rows], y_s.at[jt], y_r.at[jt],
            device_id={"cons": across}, device_id_type=MESH,
        )

    def o_copy(jt):
        rows = pl.ds(pl.multiple_of(jt * JT, JT), JT)
        mine = pl.ds(pl.multiple_of(core * half, half), half)
        return pltpu.make_async_remote_copy(
            out.at[rows, mine], out.at[rows, mine], o_s.at[jt], o_r.at[jt],
            device_id={"cons": partner}, device_id_type=MESH,
        )

    def st_copy(d):
        return pltpu.make_async_remote_copy(
            ST.at[cons], ST.at[cons], st_s.at[d], st_r.at[d],
            device_id={"cons": lax.rem(cons + d, 4)}, device_id_type=MESH,
        )

    def forward(jt):
        rows = pl.ds(pl.multiple_of(jt * JT, JT), JT)
        px_copy(jt).wait()
        YS[rows, :] = (PO[rows, :] + PR[rows, :]).astype(BF16)
        y_copy(jt).start()

    def panel(jt, carry):
        rows = pl.ds(pl.multiple_of(jt * JT, JT), JT)

        def group(g, carry):
            g0 = pl.multiple_of(g * GR, GR)
            band = pl.ds(pl.multiple_of(jt * JT + g * GR, GR), GR)
            sh = jnp.zeros((GR, 128), F32)
            dg = jnp.zeros((GR, 128), F32)
            for b in range(LI // 128):
                at = pl.ds(b * 128, 128)
                sc = E[band, at] * FL[:, at]
                SCB[pl.ds(g0, GR), at] = sc.astype(BF16)
                sh = sh + sc
                dg = dg + sc * coef[:, at]
            SH[pl.ds(g0, GR), :] = sh
            DG[pl.ds(g0, GR), :] = dg
            return carry

        lax.fori_loop(0, JT // GR, group, 0)
        acc = jnp.dot(SCB[...], WT[...], preferred_element_type=F32)
        first, second = acc[:, :half], acc[:, half:]
        PO[rows, :] = jnp.where(core == 0, first, second)
        PX[rows, :] = jnp.where(core == 0, second, first)
        px_copy(jt).start()
        ST[cons, 0:1, rows] = jnp.sum(SH[...].T, axis=0, keepdims=True)
        ST[cons, 1:2, rows] = jnp.sum(DG[...].T, axis=0, keepdims=True)

        @pl.when(jt > 0)
        def _():
            forward(jt - 1)

        return carry

    lax.fori_loop(0, nt, panel, 0)
    for d in range(1, 4):
        st_copy(d).start()
    forward(nt - 1)
    for d in range(1, 4):
        st_copy(d).wait()
    sm[0:1, :] = (ST[0, 0:1, :] + ST[1, 0:1, :] + ST[2, 0:1, :] + ST[3, 0:1, :]) / count_consumers
    ST[0, 1:2, :] = (ST[0, 1:2, :] + ST[1, 1:2, :] + ST[2, 1:2, :] + ST[3, 1:2, :]) / count_consumers
    mine = pl.ds(pl.multiple_of(core * half, half), half)
    heads = cols[:, mine]

    def finish(jt, carry):
        y_copy(jt).wait()
        for b in range(JT // block):
            r0 = pl.multiple_of(jt * JT + b * block, block)
            rows = pl.ds(r0, block)
            fb = jt * (JT // block) + b
            x = (YS[rows, :].astype(F32) + YR[rows, :].astype(F32)) / count_consumers
            diag = jnp.broadcast_to(ST[0, 1:2, rows], (half, block)).T
            mine_ids = jnp.broadcast_to(ids[:, rows], (half, block)).T
            jac = x - jnp.where(mine_ids == heads, diag, 0.0)
            m = inv[fb]
            out[rows, mine] = jnp.dot(m, jac, precision=lax.Precision.HIGHEST, preferred_element_type=F32)
            share8 = jnp.broadcast_to(sm[0:1, rows], (8, block))
            mk = lax.dot_general(share8, m, NT, precision=lax.Precision.HIGHEST, preferred_element_type=F32)
            sm[1:2, rows] = mk[0:1, :]
        o_copy(jt).start()
        return carry

    lax.fori_loop(0, nt, finish, 0)

    def drain(jt, carry):
        o_copy(jt).wait()
        return carry

    lax.fori_loop(0, nt, drain, 0)


def run_main(n, caug, tastes, coef, colpart, inverses, ids, cols, count_products, count_consumers):
    LP, LI, W = caug.shape[0], tastes.shape[0], cols.shape[1]
    KA = caug.shape[1]
    IC, JT = min(512, LI), min(256, LP)
    nc, nt = LI // IC, LP // JT
    half = W // 2
    dma = pltpu.SemaphoreType.DMA
    return pl.pallas_call(
        functools.partial(main_kernel, n, float(count_products), float(count_consumers), IC, JT, min(32, JT)),
        out_shape=(jax.ShapeDtypeStruct((LP, W), F32), jax.ShapeDtypeStruct((2, LP), F32)),
        in_specs=[VMEM] * 7,
        out_specs=(VMEM, VMEM),
        scratch_shapes=[
            pltpu.VMEM((LI, KA), BF16),
            pltpu.VMEM((JT, LI), BF16),
            pltpu.VMEM((JT, 128), F32),
            pltpu.VMEM((JT, 128), F32),
            pltpu.VMEM((LP, LI), F32),
            pltpu.VMEM((n, nc, 2, IC), F32),
            pltpu.VMEM((n, W // n, KA), F32),
            pltpu.VMEM((1, LI), F32),
            pltpu.VMEM((LI, W), BF16),
            pltpu.VMEM((LP, half), F32),
            pltpu.VMEM((LP, half), F32),
            pltpu.VMEM((LP, half), F32),
            pltpu.VMEM((LP, half), BF16),
            pltpu.VMEM((LP, half), BF16),
            pltpu.VMEM((4, 2, LP), F32),
            dma((n, nc)), dma((n, nc)), dma((n,)), dma((n,)),
            dma((nt,)), dma((nt,)), dma((nt,)), dma((nt,)),
            dma((4,)), dma((4,)), dma((nt,)), dma((nt,)),
        ],
        compiler_params=pltpu.CompilerParams(
            collective_id=7, has_side_effects=True, vmem_limit_bytes=LIMIT
        ),
    )(caug, tastes, coef, colpart, inverses, ids, cols)


def split_mean(mean):
    a = lax.reduce_precision(mean, 8, 7)
    b = lax.reduce_precision(mean - a, 8, 7)
    c = mean - a - b
    return jnp.stack([a.astype(BF16), b.astype(BF16), c.astype(BF16)], axis=1)


def lanes(count):
    return -(-count // 128) * 128


def body(tastes, price_coef, characteristics, mean_utility, panel_cols, firm_map, inverses):
    n = lax.axis_size("prod")
    LP, K = characteristics.shape
    LI = tastes.shape[0]
    W = panel_cols.shape[0]
    count_products = LP * n
    count_consumers = LI * lax.axis_size("cons")
    pp, cp = LP // n, W // n
    KA = 2 * K
    base = lax.axis_index("prod") * LP
    local = lax.iota(jnp.int32, LP)

    sid = lax.sort(firm_map)
    wanted = jnp.pad(sid.reshape(n, 1, pp), ((0, 0), (0, 0), (0, lanes(pp) - pp)))
    asked = exchange(wanted, 1)[:, 0, :pp].reshape(LP) - base

    caug = jnp.concatenate(
        [characteristics, split_mean(mean_utility), jnp.zeros((LP, KA - K - 3), BF16)], axis=1
    )
    picks = jnp.concatenate([asked, panel_cols - base])
    hot = (picks[:, None] == local[None, :]).astype(BF16)
    got = jnp.dot(hot, caug, preferred_element_type=F32).astype(BF16)
    mine = jnp.concatenate([got[:LP].reshape(n, pp, KA), got[LP:].reshape(n, cp, KA)], axis=1)
    each = pp + cp
    wide = lanes(each)
    means = jnp.pad(mine[:, :, K:K + 3].transpose(0, 2, 1), ((0, 0), (0, 0), (0, wide - each)))
    means = means.reshape(n, 3 * wide // 128, 128)
    total = each + means.shape[1]
    fill = -(-total // 32) * 32 - total
    sent = jnp.concatenate([mine[:, :, :K], means, jnp.zeros((n, fill, K), BF16)], axis=1)
    back = shared_exchange(sent, 2)
    means_back = back[:, each:total].reshape(n, 3, wide)[:, :, :each].transpose(0, 2, 1)
    both = jnp.concatenate([back[:, :each], means_back, jnp.zeros((n, each, KA - K - 3), BF16)], axis=2)
    colpart = jnp.sum(both[:, pp:].astype(F32), axis=0)
    turn = (firm_map[:, None] == sid[None, :]).astype(BF16)
    cfirm = jnp.dot(turn, both[:, :pp].reshape(LP, KA), preferred_element_type=F32).astype(BF16)
    response, sm = run_main(
        n, cfirm, tastes, price_coef[None, :], colpart, inverses,
        firm_map.astype(F32)[None, :], panel_cols.astype(F32)[None, :], count_products, count_consumers,
    )
    values = jnp.sum(jnp.where(firm_map[:, None] == sid[None, :], sm[0][:, None], 0.0), axis=0)
    values = jnp.pad(values.reshape(n, 1, pp), ((0, 0), (0, 0), (0, lanes(pp) - pp)))
    home = exchange(values, 3)[:, 0, :pp].reshape(LP)
    shares = jnp.sum(jnp.where(asked[:, None] == local[None, :], home[:, None], 0.0), axis=0)
    return shares, sm[1], response


def solution(mesh):
    return jax.shard_map(
        body,
        mesh=mesh,
        in_specs=(
            P("cons", None),
            P("cons"),
            P("prod", None),
            P("prod"),
            P(),
            P("prod"),
            P("prod", None, None),
        ),
        out_specs=(P("prod"), P("prod"), P("prod", None)),
        check_vma=False,
    )
```

```python
import functools
import jax
import jax.numpy as jnp
from jax import lax
from jax.experimental import pallas as pl
from jax.experimental.pallas import tpu as pltpu
from jax.sharding import PartitionSpec as P

F32 = jnp.float32
BF16 = jnp.bfloat16
NT = (((1,), (1,)), ((), ()))
MESH = pl.DeviceIdType.MESH
VMEM = pl.BlockSpec(memory_space=pltpu.VMEM)
LIMIT = 63 * 1024 * 1024


def turned(row):
    return jnp.broadcast_to(row, (128, 128)).T


def prep_kernel(
    n, LP, cp,
    sid, fm, chars, mean, cols,
    C, colpart, colmean, asked,
    CA, X, XM, XC, XCM, R, RM, RC, RCM,
    a_s, a_r, x_s, x_r, f_s, f_r, m_s, m_r, c_s, c_r, k_s, k_r,
):
    me = lax.axis_index("prod")
    cons = lax.axis_index("cons")
    core = lax.rem(cons, 2)
    partner = cons + 1 - 2 * core
    K = chars.shape[1]
    pad = sid.shape[2]
    base = me * LP
    barrier = pltpu.get_barrier_semaphore()
    for d in range(1, n):
        pl.semaphore_signal(barrier, inc=1, device_id={"prod": lax.rem(me + d, n)}, device_id_type=MESH)
    pl.semaphore_signal(barrier, inc=1, device_id={"cons": partner}, device_id_type=MESH)

    CA[:, :K] = chars[...]
    lane = lax.broadcasted_iota(jnp.int32, (128, K), 1)

    def split(column):
        a = column.astype(BF16).astype(F32)
        b = (column - a).astype(BF16).astype(F32)
        c = column - a - b
        return jnp.where(lane == 0, a, jnp.where(lane == 1, b, jnp.where(lane == 2, c, 0.0))).astype(BF16)

    def widen(g, carry):
        rows = pl.ds(pl.multiple_of(g * 128, 128), 128)
        CA[rows, K:] = split(turned(mean[:, rows]))
        return carry

    lax.fori_loop(0, LP // 128, widen, 0)
    pl.semaphore_wait(barrier, n)

    def send(src, dst, s, r, d):
        return pltpu.make_async_remote_copy(
            src, dst, s.at[d], r.at[d],
            device_id={"prod": lax.rem(me + d, n)}, device_id_type=MESH,
        )

    span = pad // 2
    part = pl.ds(pl.multiple_of(core * span, span), span)

    def a_copy(d):
        return send(sid.at[lax.rem(me + d, n)], asked.at[me], a_s, a_r, d)

    def x_copy(d):
        return send(X.at[lax.rem(me + d, n), part], R.at[me, part], x_s, x_r, d)

    def m_copy(d):
        return send(XM.at[lax.rem(me + d, n)], RM.at[me], m_s, m_r, d)

    def c_copy(d):
        return send(XC.at[lax.rem(me + d, n)], RC.at[me], c_s, c_r, d)

    def k_copy(d):
        return send(XCM, RCM.at[me], k_s, k_r, d)

    def f_copy(d):
        source = lax.rem(me + n - d, n)
        return pltpu.make_async_remote_copy(
            R.at[source, part], R.at[source, part], f_s.at[d], f_r.at[d],
            device_id={"cons": partner}, device_id_type=MESH,
        )

    def loop(fn, lo=1):
        def step(d, carry):
            fn(d)
            return carry
        lax.fori_loop(lo, n, step, 0)

    loop(lambda d: a_copy(d).start())
    asked[me] = sid[me]

    def pick(row):
        want = turned((row - base).astype(F32))
        spot = lax.broadcasted_iota(jnp.int32, (128, 128), 1).astype(F32)
        hot = jnp.concatenate(
            [jnp.where(want == spot + float(b * 128), 1.0, 0.0).astype(BF16) for b in range(LP // 128)], axis=1
        )
        got = jnp.dot(hot, CA[...], preferred_element_type=F32)
        t = got[:, K:].T
        return got[:, :K], t[0:1] + (t[1:2] + t[2:3])

    for g in range(cols.shape[1] // 128):
        at = pl.ds(g * 128, 128)
        rows, means = pick(cols[:, at])
        lots = 128 // cp
        XC[g * lots:(g + 1) * lots, :cp, :] = rows.reshape(lots, cp, K).astype(BF16)
        XCM[:, at] = means
    loop(lambda d: c_copy(d).start())
    loop(lambda d: k_copy(d).start())
    RC[me] = XC[me]
    RCM[me] = XCM[...]

    def answer(d, carry):
        source = lax.rem(me + n - d, n)

        @pl.when(d > 0)
        def _():
            send(sid.at[source], asked.at[source], a_s, a_r, lax.rem(n - d, n)).wait_send()
            send(sid.at[source], asked.at[source], a_s, a_r, d).wait_recv()

        for b in range(pad // 128):
            at = pl.ds(b * 128, 128)
            rows, means = pick(asked[source, :, at])
            X[source, at, :] = rows.astype(BF16)
            XM[source, :, at] = means

        @pl.when(d > 0)
        def _():
            back = lax.rem(n - d, n)
            x_copy(back).start()
            m_copy(back).start()

        return carry

    lax.fori_loop(0, n, answer, 0)
    R[me] = X[me]
    RM[me] = XM[me]

    loop(lambda d: c_copy(d).wait())
    loop(lambda d: k_copy(d).wait())
    total = RC[0, :cp, :].astype(F32)
    heads = RCM[0]
    for p in range(1, n):
        total = total + RC[p, :cp, :].astype(F32)
        heads = heads + RCM[p]
    colpart[...] = total
    colmean[...] = heads

    def relay(d):
        x_copy(d).wait()
        f_copy(d).start()

    loop(relay)
    loop(lambda d: m_copy(d).wait())
    loop(lambda d: f_copy(d).wait())
    table = R[...].reshape(n * pad, K)

    def firm(g, carry):
        rows = pl.ds(pl.multiple_of(g * 128, 128), 128)
        want = turned(fm[:, rows].astype(F32))
        hots = []
        mid = jnp.zeros((128, 128), F32)
        for p in range(n):
            for b in range(pad // 128):
                at = pl.ds(b * 128, 128)
                hit = want == sid[p, :, at].astype(F32)
                hots.append(jnp.where(hit, 1.0, 0.0).astype(BF16))
                mid = mid + jnp.where(hit, RM[p, :, at], 0.0)
        C[rows, :K] = jnp.dot(jnp.concatenate(hots, axis=1), table, preferred_element_type=F32).astype(BF16)
        C[rows, K:] = split(jnp.sum(mid, axis=1, keepdims=True))
        return carry

    lax.fori_loop(0, LP // 128, firm, 0)


def prepare(n, sid, fm, chars, mean, cols):
    LP, K = chars.shape
    W = cols.shape[1]
    cp = W // n
    room = -(-cp // 16) * 16
    pad = sid.shape[2]
    dma = pltpu.SemaphoreType.DMA
    return pl.pallas_call(
        functools.partial(prep_kernel, n, LP, cp),
        out_shape=(
            jax.ShapeDtypeStruct((LP, 2 * K), BF16),
            jax.ShapeDtypeStruct((cp, K), F32),
            jax.ShapeDtypeStruct((1, W), F32),
            jax.ShapeDtypeStruct(sid.shape, jnp.int32),
        ),
        in_specs=[VMEM] * 5,
        out_specs=(VMEM,) * 4,
        scratch_shapes=[
            pltpu.VMEM((LP, 2 * K), BF16),
            pltpu.VMEM((n, pad, K), BF16),
            pltpu.VMEM((n, 1, pad), F32),
            pltpu.VMEM((n, room, K), BF16),
            pltpu.VMEM((1, W), F32),
            pltpu.VMEM((n, pad, K), BF16),
            pltpu.VMEM((n, 1, pad), F32),
            pltpu.VMEM((n, room, K), BF16),
            pltpu.VMEM((n, 1, W), F32),
        ] + [dma((n,))] * 12,
        compiler_params=pltpu.CompilerParams(collective_id=1, has_side_effects=True),
    )(sid, fm, chars, mean, cols)


def main_kernel(
    n, count_products, count_consumers, IC, JT, GR,
    C, tastes, coef, colpart, colmean, inv, ids, cols, sid, asked,
    out, sm,
    SV, HV, T, SCB, SH, DG, E, MS, CC, FL, WT, PO, PX, PR, YS, YR, ST,
    ms_s, ms_r, cc_s, cc_r, px_s, px_r, y_s, y_r, st_s, st_r, o_s, o_r, h_s, h_r,
):
    me = lax.axis_index("prod")
    cons = lax.axis_index("cons")
    core = lax.rem(cons, 2)
    partner = cons + 1 - 2 * core
    across = lax.rem(cons + 2, 4)
    LP = C.shape[0]
    LI, K = tastes.shape
    nc, nt = LI // IC, LP // JT
    half = out.shape[1] // 2
    block = inv.shape[1]

    barrier = pltpu.get_barrier_semaphore()
    for d in range(1, n):
        pl.semaphore_signal(barrier, inc=1, device_id={"prod": lax.rem(me + d, n)}, device_id_type=MESH)
    for d in range(1, 4):
        pl.semaphore_signal(barrier, inc=1, device_id={"cons": lax.rem(cons + d, 4)}, device_id_type=MESH)
    pl.semaphore_wait(barrier, n + 2)

    def cc_copy(d):
        return pltpu.make_async_remote_copy(
            colpart, CC.at[me], cc_s.at[d], cc_r.at[d],
            device_id={"prod": lax.rem(me + d, n)}, device_id_type=MESH,
        )

    def ms_copy(d, ic):
        return pltpu.make_async_remote_copy(
            MS.at[0, ic], MS.at[d, ic], ms_s.at[d, ic], ms_r.at[d, ic],
            device_id={"prod": lax.rem(me + d, n)}, device_id_type=MESH,
        )

    def each_peer(fn):
        def step(d, carry):
            fn(d)
            return carry
        lax.fori_loop(1, n, step, 0)

    each_peer(lambda d: cc_copy(d).start())
    T[:, :K] = tastes[...]
    lane = lax.broadcasted_iota(jnp.int32, (LI, C.shape[1] - K), 1)
    T[:, K:] = jnp.where(lane < 3, 1.0, 0.0).astype(BF16)
    CC[me] = colpart[...]

    def pass_one(ic, carry):
        i0 = pl.multiple_of(ic * IC, IC)
        tb = T[pl.ds(i0, IC), :]

        def utility(jt, m8):
            rows = pl.ds(pl.multiple_of(jt * JT, JT), JT)
            u = lax.dot_general(C[rows, :], tb, NT, preferred_element_type=F32)
            E[rows, pl.ds(i0, IC)] = u
            return jnp.maximum(m8, jnp.max(u.reshape(JT // 8, 8, IC), axis=0))

        m8 = lax.fori_loop(0, nt, utility, jnp.zeros((8, IC), F32))
        m = jnp.max(m8, axis=0, keepdims=True)

        def expo(jt, s8):
            rows = pl.ds(pl.multiple_of(jt * JT, JT), JT)
            e = jnp.exp(E[rows, pl.ds(i0, IC)] - m)
            E[rows, pl.ds(i0, IC)] = e
            return s8 + jnp.sum(e.reshape(JT // 8, 8, IC), axis=0)

        s8 = lax.fori_loop(0, nt, expo, jnp.zeros((8, IC), F32))
        MS[0, ic, 0:1, :] = m
        MS[0, ic, 1:2, :] = jnp.sum(s8, axis=0, keepdims=True)
        each_peer(lambda d: ms_copy(d, ic).start())
        return carry

    lax.fori_loop(0, nc, pass_one, 0)
    each_peer(lambda d: cc_copy(d).wait())
    ccv = CC[...].reshape(CC.shape[0] * CC.shape[1], CC.shape[2]).astype(BF16)
    cm = jnp.concatenate([turned(colmean[:, g * 128:(g + 1) * 128])[:, :1] for g in range(colmean.shape[1] // 128)], axis=0)

    def weights(ic, carry):
        each_peer(lambda d: ms_copy(d, ic).wait())
        i0 = pl.multiple_of(ic * IC, IC)
        peak = MS[0, ic, 0:1, :]
        for d in range(1, n):
            peak = jnp.maximum(peak, MS[d, ic, 0:1, :])
        den = jnp.exp(-peak)
        for d in range(n):
            den = den + MS[d, ic, 1:2, :] * jnp.exp(MS[d, ic, 0:1, :] - peak)
        f = count_products / den
        FL[:, pl.ds(i0, IC)] = jnp.exp(MS[0, ic, 0:1, :] - peak) * f
        cu = lax.dot_general(ccv, tastes[pl.ds(i0, IC), :], NT, preferred_element_type=F32) + cm
        w = coef[:, pl.ds(i0, IC)] * (f * jnp.exp(cu - peak))
        WT[pl.ds(i0, IC), :] = w.T.astype(BF16)
        return carry

    lax.fori_loop(0, nc, weights, 0)

    def px_copy(jt):
        rows = pl.ds(pl.multiple_of(jt * JT, JT), JT)
        return pltpu.make_async_remote_copy(
            PX.at[rows], PR.at[rows], px_s.at[jt], px_r.at[jt],
            device_id={"cons": partner}, device_id_type=MESH,
        )

    def y_copy(jt):
        rows = pl.ds(pl.multiple_of(jt * JT, JT), JT)
        return pltpu.make_async_remote_copy(
            YS.at[rows], YR.at[rows], y_s.at[jt], y_r.at[jt],
            device_id={"cons": across}, device_id_type=MESH,
        )

    def o_copy(jt):
        rows = pl.ds(pl.multiple_of(jt * JT, JT), JT)
        mine = pl.ds(pl.multiple_of(core * half, half), half)
        return pltpu.make_async_remote_copy(
            out.at[rows, mine], out.at[rows, mine], o_s.at[jt], o_r.at[jt],
            device_id={"cons": partner}, device_id_type=MESH,
        )

    def st_copy(d):
        return pltpu.make_async_remote_copy(
            ST.at[cons], ST.at[cons], st_s.at[d], st_r.at[d],
            device_id={"cons": lax.rem(cons + d, 4)}, device_id_type=MESH,
        )

    def forward(jt):
        rows = pl.ds(pl.multiple_of(jt * JT, JT), JT)
        px_copy(jt).wait()
        YS[rows, :] = (PO[rows, :] + PR[rows, :]).astype(BF16)
        y_copy(jt).start()

    def panel(jt, carry):
        rows = pl.ds(pl.multiple_of(jt * JT, JT), JT)

        def group(g, carry):
            g0 = pl.multiple_of(g * GR, GR)
            band = pl.ds(pl.multiple_of(jt * JT + g * GR, GR), GR)
            sh = jnp.zeros((GR, 128), F32)
            dg = jnp.zeros((GR, 128), F32)
            for b in range(LI // 128):
                at = pl.ds(b * 128, 128)
                sc = E[band, at] * FL[:, at]
                SCB[pl.ds(g0, GR), at] = sc.astype(BF16)
                sh = sh + sc
                dg = dg + sc * coef[:, at]
            SH[pl.ds(g0, GR), :] = sh
            DG[pl.ds(g0, GR), :] = dg
            return carry

        lax.fori_loop(0, JT // GR, group, 0)
        acc = jnp.dot(SCB[...], WT[...], preferred_element_type=F32)
        first, second = acc[:, :half], acc[:, half:]
        PO[rows, :] = jnp.where(core == 0, first, second)
        PX[rows, :] = jnp.where(core == 0, second, first)
        px_copy(jt).start()
        ST[cons, 0:1, rows] = jnp.sum(SH[...].T, axis=0, keepdims=True)
        ST[cons, 1:2, rows] = jnp.sum(DG[...].T, axis=0, keepdims=True)

        @pl.when(jt > 0)
        def _():
            forward(jt - 1)

        return carry

    lax.fori_loop(0, nt, panel, 0)
    for d in range(1, 4):
        st_copy(d).start()
    forward(nt - 1)
    for d in range(1, 4):
        st_copy(d).wait()
    sm[0:1, :] = (ST[0, 0:1, :] + ST[1, 0:1, :] + ST[2, 0:1, :] + ST[3, 0:1, :]) / count_consumers
    ST[0, 1:2, :] = (ST[0, 1:2, :] + ST[1, 1:2, :] + ST[2, 1:2, :] + ST[3, 1:2, :]) / count_consumers
    pad = sid.shape[2]
    spans = [(p, b) for p in range(n) for b in range(pad // 128)]

    def sorted_step(g, carry):
        rows = pl.ds(pl.multiple_of(g * 128, 128), 128)
        want = turned(ids[:, rows])
        share = turned(sm[0:1, rows])
        for p, b in spans:
            at = pl.ds(b * 128, 128)
            hit = jnp.where(want == sid[p, :, at].astype(F32), share, 0.0)
            SV[p, :, at] += jnp.sum(hit, axis=0, keepdims=True)
        return carry

    SV[...] = jnp.zeros_like(SV)
    lax.fori_loop(0, LP // 128, sorted_step, 0)

    def h_copy(d):
        peer = lax.rem(me + d, n)
        return pltpu.make_async_remote_copy(
            SV.at[peer], HV.at[me], h_s.at[d], h_r.at[d],
            device_id={"prod": peer}, device_id_type=MESH,
        )

    each_peer(lambda d: h_copy(d).start())
    HV[me] = SV[me]
    mine = pl.ds(pl.multiple_of(core * half, half), half)
    heads = cols[:, mine]

    def finish(jt, carry):
        y_copy(jt).wait()
        for b in range(JT // block):
            r0 = pl.multiple_of(jt * JT + b * block, block)
            rows = pl.ds(r0, block)
            fb = jt * (JT // block) + b
            x = (YS[rows, :].astype(F32) + YR[rows, :].astype(F32)) / count_consumers
            diag = jnp.broadcast_to(ST[0, 1:2, rows], (half, block)).T
            mine_ids = jnp.broadcast_to(ids[:, rows], (half, block)).T
            jac = x - jnp.where(mine_ids == heads, diag, 0.0)
            m = inv[fb]
            out[rows, mine] = jnp.dot(m, jac, precision=lax.Precision.HIGHEST, preferred_element_type=F32)
            share8 = jnp.broadcast_to(sm[0:1, rows], (8, block))
            mk = lax.dot_general(share8, m, NT, precision=lax.Precision.HIGHEST, preferred_element_type=F32)
            sm[1:2, rows] = mk[0:1, :]
        o_copy(jt).start()
        return carry

    lax.fori_loop(0, nt, finish, 0)

    each_peer(lambda d: h_copy(d).wait())
    sm[2:3, :] = jnp.zeros((1, LP), F32)

    def home_step(p, carry):
        for b in range(pad // 128):
            at = pl.ds(b * 128, 128)
            want = turned((asked[p, :, at] - me * LP).astype(F32))
            share = turned(HV[p, :, at])
            spot = lax.broadcasted_iota(jnp.int32, (128, 128), 1).astype(F32)
            for g in range(LP // 128):
                to = pl.ds(g * 128, 128)
                hit = jnp.where(want == spot + float(g * 128), share, 0.0)
                sm[2:3, to] += jnp.sum(hit, axis=0, keepdims=True)
        return carry

    lax.fori_loop(0, n, home_step, 0)

    def drain(jt, carry):
        o_copy(jt).wait()
        return carry

    lax.fori_loop(0, nt, drain, 0)


def run_main(n, caug, tastes, coef, colpart, colmean, inverses, ids, cols, sid, asked, count_products, count_consumers):
    LP, LI, W = caug.shape[0], tastes.shape[0], cols.shape[1]
    KA = caug.shape[1]
    IC, JT = min(512, LI), min(256, LP)
    nc, nt = LI // IC, LP // JT
    half = W // 2
    dma = pltpu.SemaphoreType.DMA
    return pl.pallas_call(
        functools.partial(main_kernel, n, float(count_products), float(count_consumers), IC, JT, min(32, JT)),
        out_shape=(jax.ShapeDtypeStruct((LP, W), F32), jax.ShapeDtypeStruct((3, LP), F32)),
        in_specs=[VMEM] * 10,
        out_specs=(VMEM, VMEM),
        scratch_shapes=[
            pltpu.VMEM(sid.shape, F32),
            pltpu.VMEM(sid.shape, F32),
            pltpu.VMEM((LI, KA), BF16),
            pltpu.VMEM((JT, LI), BF16),
            pltpu.VMEM((JT, 128), F32),
            pltpu.VMEM((JT, 128), F32),
            pltpu.VMEM((LP, LI), F32),
            pltpu.VMEM((n, nc, 2, IC), F32),
            pltpu.VMEM((n, W // n, KA // 2), F32),
            pltpu.VMEM((1, LI), F32),
            pltpu.VMEM((LI, W), BF16),
            pltpu.VMEM((LP, half), F32),
            pltpu.VMEM((LP, half), F32),
            pltpu.VMEM((LP, half), F32),
            pltpu.VMEM((LP, half), BF16),
            pltpu.VMEM((LP, half), BF16),
            pltpu.VMEM((4, 2, LP), F32),
            dma((n, nc)), dma((n, nc)), dma((n,)), dma((n,)),
            dma((nt,)), dma((nt,)), dma((nt,)), dma((nt,)),
            dma((4,)), dma((4,)), dma((nt,)), dma((nt,)), dma((n,)), dma((n,)),
        ],
        compiler_params=pltpu.CompilerParams(
            collective_id=7, has_side_effects=True, vmem_limit_bytes=LIMIT
        ),
    )(caug, tastes, coef, colpart, colmean, inverses, ids, cols, sid, asked)


def lanes(count):
    return -(-count // 128) * 128


def body(tastes, price_coef, characteristics, mean_utility, panel_cols, firm_map, inverses):
    n = lax.axis_size("prod")
    LP, K = characteristics.shape
    LI = tastes.shape[0]
    W = panel_cols.shape[0]
    count_products = LP * n
    count_consumers = LI * lax.axis_size("cons")
    pp = LP // n
    sid = jnp.pad(
        lax.sort(firm_map).reshape(n, 1, pp), ((0, 0), (0, 0), (0, lanes(pp) - pp)), constant_values=-1
    )
    cfirm, colpart, colmean, asked = prepare(
        n, sid, firm_map[None, :], characteristics, mean_utility[None, :], panel_cols[None, :]
    )
    response, sm = run_main(
        n, cfirm, tastes, price_coef[None, :], colpart, colmean, inverses,
        firm_map.astype(F32)[None, :], panel_cols.astype(F32)[None, :], sid, asked,
        count_products, count_consumers,
    )
    return sm[2], sm[1], response


def solution(mesh):
    return jax.shard_map(
        body,
        mesh=mesh,
        in_specs=(
            P("cons", None),
            P("cons"),
            P("prod", None),
            P("prod"),
            P(),
            P("prod"),
            P("prod", None, None),
        ),
        out_specs=(P("prod"), P("prod"), P("prod", None)),
        check_vma=False,
    )
```

```python
import functools
import jax
import jax.numpy as jnp
from jax import lax
from jax.experimental import pallas as pl
from jax.experimental.pallas import tpu as pltpu
from jax.sharding import PartitionSpec as P

F32 = jnp.float32
BF16 = jnp.bfloat16
NT = (((1,), (1,)), ((), ()))
MESH = pl.DeviceIdType.MESH
VMEM = pl.BlockSpec(memory_space=pltpu.VMEM)
LIMIT = 63 * 1024 * 1024


def turned(row):
    return jnp.broadcast_to(row, (128, 128)).T


def prep_kernel(
    n, LP, cp,
    sid, fm, chars, mean, cols,
    C, colpart, colmean, asked,
    CA, X, XM, XC, XCM, R, RM, RC, RCM,
    a_s, a_r, x_s, x_r, f_s, f_r, m_s, m_r, c_s, c_r, k_s, k_r,
):
    me = lax.axis_index("prod")
    cons = lax.axis_index("cons")
    core = lax.rem(cons, 2)
    partner = cons + 1 - 2 * core
    K = chars.shape[1]
    pad = sid.shape[2]
    base = me * LP
    barrier = pltpu.get_barrier_semaphore()
    for d in range(1, n):
        pl.semaphore_signal(barrier, inc=1, device_id={"prod": lax.rem(me + d, n)}, device_id_type=MESH)
    pl.semaphore_signal(barrier, inc=1, device_id={"cons": partner}, device_id_type=MESH)

    CA[:, :K] = chars[...]
    lane = lax.broadcasted_iota(jnp.int32, (128, K), 1)

    def split(column):
        a = column.astype(BF16).astype(F32)
        b = (column - a).astype(BF16).astype(F32)
        c = column - a - b
        return jnp.where(lane == 0, a, jnp.where(lane == 1, b, jnp.where(lane == 2, c, 0.0))).astype(BF16)

    def widen(g, carry):
        rows = pl.ds(pl.multiple_of(g * 128, 128), 128)
        CA[rows, K:] = split(turned(mean[:, rows]))
        return carry

    lax.fori_loop(0, LP // 128, widen, 0)
    pl.semaphore_wait(barrier, n)

    def send(src, dst, s, r, d):
        return pltpu.make_async_remote_copy(
            src, dst, s.at[d], r.at[d],
            device_id={"prod": lax.rem(me + d, n)}, device_id_type=MESH,
        )

    span = pad // 2
    part = pl.ds(pl.multiple_of(core * span, span), span)

    def a_copy(d):
        return send(sid.at[lax.rem(me + d, n)], asked.at[me], a_s, a_r, d)

    def x_copy(d):
        return send(X.at[lax.rem(me + d, n), part], R.at[me, part], x_s, x_r, d)

    def m_copy(d):
        return send(XM.at[lax.rem(me + d, n)], RM.at[me], m_s, m_r, d)

    def c_copy(d):
        return send(XC.at[lax.rem(me + d, n)], RC.at[me], c_s, c_r, d)

    def k_copy(d):
        return send(XCM, RCM.at[me], k_s, k_r, d)

    def f_copy(d):
        source = lax.rem(me + n - d, n)
        return pltpu.make_async_remote_copy(
            R.at[source, part], R.at[source, part], f_s.at[d], f_r.at[d],
            device_id={"cons": partner}, device_id_type=MESH,
        )

    def loop(fn, lo=1):
        def step(d, carry):
            fn(d)
            return carry
        lax.fori_loop(lo, n, step, 0)

    loop(lambda d: a_copy(d).start())
    asked[me] = sid[me]

    def pick(row):
        want = turned((row - base).astype(F32))
        spot = lax.broadcasted_iota(jnp.int32, (128, 128), 1).astype(F32)
        hot = jnp.concatenate(
            [jnp.where(want == spot + float(b * 128), 1.0, 0.0).astype(BF16) for b in range(LP // 128)], axis=1
        )
        got = jnp.dot(hot, CA[...], preferred_element_type=F32)
        t = got[:, K:].T
        return got[:, :K], t[0:1] + (t[1:2] + t[2:3])

    for g in range(cols.shape[1] // 128):
        at = pl.ds(g * 128, 128)
        rows, means = pick(cols[:, at])
        lots = 128 // cp
        XC[g * lots:(g + 1) * lots, :cp, :] = rows.reshape(lots, cp, K).astype(BF16)
        XCM[:, at] = means
    loop(lambda d: c_copy(d).start())
    loop(lambda d: k_copy(d).start())
    RC[me] = XC[me]
    RCM[me] = XCM[...]

    def answer(d, carry):
        source = lax.rem(me + n - d, n)

        @pl.when(d > 0)
        def _():
            send(sid.at[source], asked.at[source], a_s, a_r, lax.rem(n - d, n)).wait_send()
            send(sid.at[source], asked.at[source], a_s, a_r, d).wait_recv()

        for b in range(pad // 128):
            at = pl.ds(b * 128, 128)
            rows, means = pick(asked[source, :, at])
            X[source, at, :] = rows.astype(BF16)
            XM[source, :, at] = means

        @pl.when(d > 0)
        def _():
            back = lax.rem(n - d, n)
            x_copy(back).start()
            m_copy(back).start()

        return carry

    lax.fori_loop(0, n, answer, 0)
    R[me] = X[me]
    RM[me] = XM[me]

    loop(lambda d: c_copy(d).wait())
    loop(lambda d: k_copy(d).wait())
    total = RC[0, :cp, :].astype(F32)
    heads = RCM[0]
    for p in range(1, n):
        total = total + RC[p, :cp, :].astype(F32)
        heads = heads + RCM[p]
    colpart[...] = total
    colmean[...] = heads

    def relay(d):
        x_copy(d).wait()
        f_copy(d).start()

    loop(relay)
    loop(lambda d: m_copy(d).wait())
    loop(lambda d: f_copy(d).wait())
    table = R[...].reshape(n * pad, K)

    def firm(g, carry):
        bands = []
        for h in range(2):
            rows = pl.ds(pl.multiple_of(g * 256 + h * 128, 128), 128)
            want = turned(fm[:, rows].astype(F32))
            hots = []
            mid = jnp.zeros((128, 128), F32)
            for p in range(n):
                for b in range(pad // 128):
                    at = pl.ds(b * 128, 128)
                    hit = want == sid[p, :, at].astype(F32)
                    hots.append(jnp.where(hit, 1.0, 0.0).astype(BF16))
                    mid = mid + jnp.where(hit, RM[p, :, at], 0.0)
            bands.append(jnp.concatenate(hots, axis=1))
            C[rows, K:] = split(jnp.sum(mid, axis=1, keepdims=True))
        rows = pl.ds(pl.multiple_of(g * 256, 256), 256)
        C[rows, :K] = jnp.dot(jnp.concatenate(bands, axis=0), table, preferred_element_type=F32).astype(BF16)
        return carry

    lax.fori_loop(0, LP // 256, firm, 0)


def prepare(n, sid, fm, chars, mean, cols):
    LP, K = chars.shape
    W = cols.shape[1]
    cp = W // n
    room = -(-cp // 16) * 16
    pad = sid.shape[2]
    dma = pltpu.SemaphoreType.DMA
    return pl.pallas_call(
        functools.partial(prep_kernel, n, LP, cp),
        out_shape=(
            jax.ShapeDtypeStruct((LP, 2 * K), BF16),
            jax.ShapeDtypeStruct((cp, K), F32),
            jax.ShapeDtypeStruct((1, W), F32),
            jax.ShapeDtypeStruct(sid.shape, jnp.int32),
        ),
        in_specs=[VMEM] * 5,
        out_specs=(VMEM,) * 4,
        scratch_shapes=[
            pltpu.VMEM((LP, 2 * K), BF16),
            pltpu.VMEM((n, pad, K), BF16),
            pltpu.VMEM((n, 1, pad), F32),
            pltpu.VMEM((n, room, K), BF16),
            pltpu.VMEM((1, W), F32),
            pltpu.VMEM((n, pad, K), BF16),
            pltpu.VMEM((n, 1, pad), F32),
            pltpu.VMEM((n, room, K), BF16),
            pltpu.VMEM((n, 1, W), F32),
        ] + [dma((n,))] * 12,
        compiler_params=pltpu.CompilerParams(collective_id=1, has_side_effects=True),
    )(sid, fm, chars, mean, cols)


def main_kernel(
    n, count_products, count_consumers, IC, JT, GR,
    C, tastes, coef, colpart, colmean, inv, ids, cols, sid, asked,
    out, sm,
    SV, HV, T, SCB, SH, DG, E, MS, CC, FL, WT, PO, PX, PR, YS, YR, ST,
    ms_s, ms_r, cc_s, cc_r, px_s, px_r, y_s, y_r, st_s, st_r, o_s, o_r, h_s, h_r,
):
    me = lax.axis_index("prod")
    cons = lax.axis_index("cons")
    core = lax.rem(cons, 2)
    partner = cons + 1 - 2 * core
    across = lax.rem(cons + 2, 4)
    LP = C.shape[0]
    LI, K = tastes.shape
    nc, nt = LI // IC, LP // JT
    half = out.shape[1] // 2
    block = inv.shape[1]

    barrier = pltpu.get_barrier_semaphore()
    for d in range(1, n):
        pl.semaphore_signal(barrier, inc=1, device_id={"prod": lax.rem(me + d, n)}, device_id_type=MESH)
    for d in range(1, 4):
        pl.semaphore_signal(barrier, inc=1, device_id={"cons": lax.rem(cons + d, 4)}, device_id_type=MESH)
    pl.semaphore_wait(barrier, n + 2)

    def cc_copy(d):
        return pltpu.make_async_remote_copy(
            colpart, CC.at[me], cc_s.at[d], cc_r.at[d],
            device_id={"prod": lax.rem(me + d, n)}, device_id_type=MESH,
        )

    def ms_copy(d, ic):
        return pltpu.make_async_remote_copy(
            MS.at[0, ic], MS.at[d, ic], ms_s.at[d, ic], ms_r.at[d, ic],
            device_id={"prod": lax.rem(me + d, n)}, device_id_type=MESH,
        )

    def each_peer(fn):
        def step(d, carry):
            fn(d)
            return carry
        lax.fori_loop(1, n, step, 0)

    each_peer(lambda d: cc_copy(d).start())
    T[:, :K] = tastes[...]
    lane = lax.broadcasted_iota(jnp.int32, (LI, C.shape[1] - K), 1)
    T[:, K:] = jnp.where(lane < 3, 1.0, 0.0).astype(BF16)
    CC[me] = colpart[...]

    def pass_one(ic, carry):
        i0 = pl.multiple_of(ic * IC, IC)
        tb = T[pl.ds(i0, IC), :]

        def utility(jt, m8):
            rows = pl.ds(pl.multiple_of(jt * JT, JT), JT)
            u = lax.dot_general(C[rows, :], tb, NT, preferred_element_type=F32)
            E[rows, pl.ds(i0, IC)] = u
            return jnp.maximum(m8, jnp.max(u.reshape(JT // 8, 8, IC), axis=0))

        m8 = lax.fori_loop(0, nt, utility, jnp.zeros((8, IC), F32))
        m = jnp.max(m8, axis=0, keepdims=True)

        def expo(jt, s8):
            rows = pl.ds(pl.multiple_of(jt * JT, JT), JT)
            e = jnp.exp(E[rows, pl.ds(i0, IC)] - m)
            E[rows, pl.ds(i0, IC)] = e
            return s8 + jnp.sum(e.reshape(JT // 8, 8, IC), axis=0)

        s8 = lax.fori_loop(0, nt, expo, jnp.zeros((8, IC), F32))
        MS[0, ic, 0:1, :] = m
        MS[0, ic, 1:2, :] = jnp.sum(s8, axis=0, keepdims=True)
        each_peer(lambda d: ms_copy(d, ic).start())
        return carry

    lax.fori_loop(0, nc, pass_one, 0)
    each_peer(lambda d: cc_copy(d).wait())
    ccv = CC[...].reshape(CC.shape[0] * CC.shape[1], CC.shape[2]).astype(BF16)
    cm = jnp.concatenate([turned(colmean[:, g * 128:(g + 1) * 128])[:, :1] for g in range(colmean.shape[1] // 128)], axis=0)

    def weights(ic, carry):
        each_peer(lambda d: ms_copy(d, ic).wait())
        i0 = pl.multiple_of(ic * IC, IC)
        peak = MS[0, ic, 0:1, :]
        for d in range(1, n):
            peak = jnp.maximum(peak, MS[d, ic, 0:1, :])
        den = jnp.exp(-peak)
        for d in range(n):
            den = den + MS[d, ic, 1:2, :] * jnp.exp(MS[d, ic, 0:1, :] - peak)
        f = count_products / den
        FL[:, pl.ds(i0, IC)] = jnp.exp(MS[0, ic, 0:1, :] - peak) * f
        cu = lax.dot_general(ccv, tastes[pl.ds(i0, IC), :], NT, preferred_element_type=F32) + cm
        w = coef[:, pl.ds(i0, IC)] * (f * jnp.exp(cu - peak))
        WT[pl.ds(i0, IC), :] = w.T.astype(BF16)
        return carry

    lax.fori_loop(0, nc, weights, 0)

    def px_copy(jt):
        rows = pl.ds(pl.multiple_of(jt * JT, JT), JT)
        return pltpu.make_async_remote_copy(
            PX.at[rows], PR.at[rows], px_s.at[jt], px_r.at[jt],
            device_id={"cons": partner}, device_id_type=MESH,
        )

    def y_copy(jt):
        rows = pl.ds(pl.multiple_of(jt * JT, JT), JT)
        return pltpu.make_async_remote_copy(
            YS.at[rows], YR.at[rows], y_s.at[jt], y_r.at[jt],
            device_id={"cons": across}, device_id_type=MESH,
        )

    def o_copy(jt):
        rows = pl.ds(pl.multiple_of(jt * JT, JT), JT)
        mine = pl.ds(pl.multiple_of(core * half, half), half)
        return pltpu.make_async_remote_copy(
            out.at[rows, mine], out.at[rows, mine], o_s.at[jt], o_r.at[jt],
            device_id={"cons": partner}, device_id_type=MESH,
        )

    def st_copy(d):
        return pltpu.make_async_remote_copy(
            ST.at[cons], ST.at[cons], st_s.at[d], st_r.at[d],
            device_id={"cons": lax.rem(cons + d, 4)}, device_id_type=MESH,
        )

    def forward(jt):
        rows = pl.ds(pl.multiple_of(jt * JT, JT), JT)
        px_copy(jt).wait()
        YS[rows, :] = (PO[rows, :] + PR[rows, :]).astype(BF16)
        y_copy(jt).start()

    def panel(jt, carry):
        rows = pl.ds(pl.multiple_of(jt * JT, JT), JT)

        def group(g, carry):
            g0 = pl.multiple_of(g * GR, GR)
            band = pl.ds(pl.multiple_of(jt * JT + g * GR, GR), GR)
            sh = jnp.zeros((GR, 128), F32)
            dg = jnp.zeros((GR, 128), F32)
            for b in range(LI // 128):
                at = pl.ds(b * 128, 128)
                sc = E[band, at] * FL[:, at]
                SCB[pl.ds(g0, GR), at] = sc.astype(BF16)
                sh = sh + sc
                dg = dg + sc * coef[:, at]
            SH[pl.ds(g0, GR), :] = sh
            DG[pl.ds(g0, GR), :] = dg
            return carry

        lax.fori_loop(0, JT // GR, group, 0)
        acc = jnp.dot(SCB[...], WT[...], preferred_element_type=F32)
        first, second = acc[:, :half], acc[:, half:]
        PO[rows, :] = jnp.where(core == 0, first, second)
        PX[rows, :] = jnp.where(core == 0, second, first)
        px_copy(jt).start()
        ST[cons, 0:1, rows] = jnp.sum(SH[...].T, axis=0, keepdims=True)
        ST[cons, 1:2, rows] = jnp.sum(DG[...].T, axis=0, keepdims=True)

        @pl.when(jt > 0)
        def _():
            forward(jt - 1)

        return carry

    lax.fori_loop(0, nt, panel, 0)
    for d in range(1, 4):
        st_copy(d).start()
    forward(nt - 1)
    for d in range(1, 4):
        st_copy(d).wait()
    sm[0:1, :] = (ST[0, 0:1, :] + ST[1, 0:1, :] + ST[2, 0:1, :] + ST[3, 0:1, :]) / count_consumers
    ST[0, 1:2, :] = (ST[0, 1:2, :] + ST[1, 1:2, :] + ST[2, 1:2, :] + ST[3, 1:2, :]) / count_consumers
    pad = sid.shape[2]
    spans = [(p, b) for p in range(n) for b in range(pad // 128)]

    def sorted_step(g, carry):
        rows = pl.ds(pl.multiple_of(g * 128, 128), 128)
        want = turned(ids[:, rows].astype(F32))
        share = turned(sm[0:1, rows])
        for p, b in spans:
            at = pl.ds(b * 128, 128)
            hit = jnp.where(want == sid[p, :, at].astype(F32), share, 0.0)
            SV[p, :, at] += jnp.sum(hit, axis=0, keepdims=True)
        return carry

    SV[...] = jnp.zeros_like(SV)
    lax.fori_loop(0, LP // 128, sorted_step, 0)

    def h_copy(d):
        peer = lax.rem(me + d, n)
        return pltpu.make_async_remote_copy(
            SV.at[peer], HV.at[me], h_s.at[d], h_r.at[d],
            device_id={"prod": peer}, device_id_type=MESH,
        )

    each_peer(lambda d: h_copy(d).start())
    HV[me] = SV[me]
    mine = pl.ds(pl.multiple_of(core * half, half), half)
    heads = cols[:, mine].astype(F32)

    def finish(jt, carry):
        y_copy(jt).wait()
        for b in range(JT // block):
            r0 = pl.multiple_of(jt * JT + b * block, block)
            rows = pl.ds(r0, block)
            fb = jt * (JT // block) + b
            x = (YS[rows, :].astype(F32) + YR[rows, :].astype(F32)) / count_consumers
            diag = jnp.broadcast_to(ST[0, 1:2, rows], (half, block)).T
            mine_ids = jnp.broadcast_to(ids[:, rows].astype(F32), (half, block)).T
            jac = x - jnp.where(mine_ids == heads, diag, 0.0)
            m = inv[fb]
            out[rows, mine] = jnp.dot(m, jac, precision=lax.Precision.HIGHEST, preferred_element_type=F32)
            share8 = jnp.broadcast_to(sm[0:1, rows], (8, block))
            mk = lax.dot_general(share8, m, NT, precision=lax.Precision.HIGHEST, preferred_element_type=F32)
            sm[1:2, rows] = mk[0:1, :]
        o_copy(jt).start()
        return carry

    lax.fori_loop(0, nt, finish, 0)

    each_peer(lambda d: h_copy(d).wait())
    sm[2:3, :] = jnp.zeros((1, LP), F32)

    def home_step(p, carry):
        for b in range(pad // 128):
            at = pl.ds(b * 128, 128)
            want = turned((asked[p, :, at] - me * LP).astype(F32))
            share = turned(HV[p, :, at])
            spot = lax.broadcasted_iota(jnp.int32, (128, 128), 1).astype(F32)
            for g in range(LP // 128):
                to = pl.ds(g * 128, 128)
                hit = jnp.where(want == spot + float(g * 128), share, 0.0)
                sm[2:3, to] += jnp.sum(hit, axis=0, keepdims=True)
        return carry

    lax.fori_loop(0, n, home_step, 0)

    def drain(jt, carry):
        o_copy(jt).wait()
        return carry

    lax.fori_loop(0, nt, drain, 0)


def run_main(n, caug, tastes, coef, colpart, colmean, inverses, ids, cols, sid, asked, count_products, count_consumers):
    LP, LI, W = caug.shape[0], tastes.shape[0], cols.shape[1]
    KA = caug.shape[1]
    IC, JT = min(512, LI), min(512, LP)
    nc, nt = LI // IC, LP // JT
    half = W // 2
    dma = pltpu.SemaphoreType.DMA
    return pl.pallas_call(
        functools.partial(main_kernel, n, float(count_products), float(count_consumers), IC, JT, min(32, JT)),
        out_shape=(jax.ShapeDtypeStruct((LP, W), F32), jax.ShapeDtypeStruct((3, LP), F32)),
        in_specs=[VMEM] * 10,
        out_specs=(VMEM, VMEM),
        scratch_shapes=[
            pltpu.VMEM(sid.shape, F32),
            pltpu.VMEM(sid.shape, F32),
            pltpu.VMEM((LI, KA), BF16),
            pltpu.VMEM((JT, LI), BF16),
            pltpu.VMEM((JT, 128), F32),
            pltpu.VMEM((JT, 128), F32),
            pltpu.VMEM((LP, LI), F32),
            pltpu.VMEM((n, nc, 2, IC), F32),
            pltpu.VMEM((n, W // n, KA // 2), F32),
            pltpu.VMEM((1, LI), F32),
            pltpu.VMEM((LI, W), BF16),
            pltpu.VMEM((LP, half), F32),
            pltpu.VMEM((LP, half), F32),
            pltpu.VMEM((LP, half), F32),
            pltpu.VMEM((LP, half), BF16),
            pltpu.VMEM((LP, half), BF16),
            pltpu.VMEM((4, 2, LP), F32),
            dma((n, nc)), dma((n, nc)), dma((n,)), dma((n,)),
            dma((nt,)), dma((nt,)), dma((nt,)), dma((nt,)),
            dma((4,)), dma((4,)), dma((nt,)), dma((nt,)), dma((n,)), dma((n,)),
        ],
        compiler_params=pltpu.CompilerParams(
            collective_id=7, has_side_effects=True, vmem_limit_bytes=LIMIT
        ),
    )(caug, tastes, coef, colpart, colmean, inverses, ids, cols, sid, asked)


def lanes(count):
    return -(-count // 128) * 128


def body(tastes, price_coef, characteristics, mean_utility, panel_cols, firm_map, inverses):
    n = lax.axis_size("prod")
    LP, K = characteristics.shape
    LI = tastes.shape[0]
    W = panel_cols.shape[0]
    count_products = LP * n
    count_consumers = LI * lax.axis_size("cons")
    pp = LP // n
    sid = jnp.pad(
        lax.sort(firm_map).reshape(n, 1, pp), ((0, 0), (0, 0), (0, lanes(pp) - pp)), constant_values=-1
    )
    cfirm, colpart, colmean, asked = prepare(
        n, sid, firm_map[None, :], characteristics, mean_utility[None, :], panel_cols[None, :]
    )
    response, sm = run_main(
        n, cfirm, tastes, price_coef[None, :], colpart, colmean, inverses,
        firm_map[None, :], panel_cols[None, :], sid, asked,
        count_products, count_consumers,
    )
    return sm[2], sm[1], response


def solution(mesh):
    return jax.shard_map(
        body,
        mesh=mesh,
        in_specs=(
            P("cons", None),
            P("cons"),
            P("prod", None),
            P("prod"),
            P(),
            P("prod"),
            P("prod", None, None),
        ),
        out_specs=(P("prod"), P("prod"), P("prod", None)),
        check_vma=False,
    )
```
